32 devices in a mesh: dp: 4 (over y, x), fsdp: 2 (over core), seq: 4 (over z).
Axes of the slice: x: 2, y: 2, z: 4, core: 2. Of those that a mesh axis runs over, the one named last changes fastest.
Arguments:
- queries: bfloat16 [8, 512, 4096], P(('dp', 'fsdp'), 'seq'), may hold values from -80 to 80
- keys: bfloat16 [8, 512, 512], P(('dp', 'fsdp'), 'seq'), may hold values from -4 to 4
- values: bfloat16 [8, 512, 512], P(('dp', 'fsdp'), 'seq'), may hold values from -5 to 5
- upstream_grad: bfloat16 [8, 512, 4096], P(('dp', 'fsdp'), 'seq'), may hold values from -2 to 2
- adapter_in: bfloat16 [8, 512, 128], P(('dp', 'fsdp'), 'seq'), may hold values from -6 to 6
- doc_lengths: int32 [8, 8], P(('dp', 'fsdp')), may hold values from 1 to 128, 512 in all within a row
Outputs:
- d_lora_b: float32 [128, 4096], P('fsdp', 'seq')
The draws below stay inside these ranges and needn't reach their ends.
Inputs may be any that keep to these rules, and one draw needn't show every extreme that they name: `doc_lengths`: each row holds the lengths of 8 documents of one sequence; they sum to 512 and the longest is exactly 128.
All inputs are finite; a program needn't handle non-finite values.
Results may differ from the reference program's by a relative error of at most 0.0055.
Values may be sent and summed in bfloat16 or wider, within the bound.
A program may use at most 64 MiB of HBM per device.

```python
import math
import jax
import jax.numpy as jnp
import numpy as np
from jax import lax

HEAD_SIZE = 128
QUERY_HEAD_COUNT = 32
KEY_VALUE_HEADS = 4
R = 128
NDOC = 8
TOKENS_PER_SEQ = 512
DOC_MAX = 128
SEQUENCE_TOTAL = 8
GROUP = 8


def paired_rows(key):
    base_offset = jax.random.fold_in(key, 11)
    key_row_block = jnp.clip(jax.random.normal(jax.random.fold_in(base_offset, 1), (SEQUENCE_TOTAL, TOKENS_PER_SEQ, KEY_VALUE_HEADS, HEAD_SIZE), jnp.float32), -4.0, 4.0)
    query_rows = jnp.clip(jax.random.normal(jax.random.fold_in(base_offset, 2), (SEQUENCE_TOTAL, TOKENS_PER_SEQ, QUERY_HEAD_COUNT, HEAD_SIZE), jnp.float32), -4.0, 4.0)
    return (key_row_block, query_rows)


def draw_queries(key, part):
    key_row_block, query_rows = paired_rows(key)
    return query_rows.reshape(SEQUENCE_TOTAL, TOKENS_PER_SEQ, QUERY_HEAD_COUNT * HEAD_SIZE).astype(jnp.bfloat16)


def draw_keys(key, part):
    key_row_block, query_rows = paired_rows(key)
    return key_row_block.reshape(SEQUENCE_TOTAL, TOKENS_PER_SEQ, KEY_VALUE_HEADS * HEAD_SIZE).astype(jnp.bfloat16)


def levels(stream_key, extent, shards, smallest, high):
    def one(dim, parts):
        steps = jax.random.uniform(jax.random.fold_in(jax.random.fold_in(stream_key, 6), dim), (parts,), jnp.float32, smallest / len(shards), high / len(shards))
        return jnp.repeat(jnp.exp(steps), extent[dim] // parts).reshape((-1,) + (1,) * (len(extent) - dim - 1))

    gain = one(*shards[0])
    for cut in shards[1:]:
        gain = gain * one(*cut)
    return gain


def profile(count, total, most, lean):
    weights = [(1 << 20) // math.isqrt(standing ** lean) + 1 for standing in range(2, count + 1)]
    surplus, counts = total - most - (count - 1), [1] * (count - 1)
    while surplus > 0:
        movable = [i for i in range(count - 1) if counts[i] < most]
        pool, left = sum([weights[i] for i in movable]), surplus
        for i in movable:
            addition = min(most - counts[i], max(1, left * weights[i] // pool), surplus)
            counts[i] = counts[i] + addition
            surplus = surplus - addition
    return np.array([most] + counts)


def ragged(own_key, amount, total, most, slope):
    if amount == 2:
        one = jax.random.randint(own_key, (), max(1, total - most), min(most, total - 1) + 1)
        return jnp.stack([one, total - one])
    sizes = jnp.asarray(profile(amount, total, most, slope), jnp.int32)
    pairs = (amount - 1) // 2
    donor, sink = sizes[1:1 + 2 * pairs:2], sizes[2:2 + 2 * pairs:2]
    slack = jnp.minimum(donor - 1, most - sink)
    moved = jax.random.randint(jax.random.fold_in(own_key, 1), (pairs,), 0, 1 << 20) % (slack + 1)
    sizes = sizes.at[1:1 + 2 * pairs:2].set(donor - moved).at[2:2 + 2 * pairs:2].set(sink + moved)
    return sizes[jax.random.permutation(jax.random.fold_in(own_key, 2), amount)]


def scatter_about(stream_key, dims, spread, most, pieces=(), held_as=jnp.bfloat16):
    values = jax.random.normal(stream_key, dims, jnp.float32) * spread
    if len(pieces) > 0:
        values = levels(stream_key, dims, pieces, -0.22, 0.18) * values
    return jnp.clip(values, min=-most, max=most).astype(held_as)


def setup_inputs(seed: int = 0) -> dict:
    seeds = jax.random.split(jax.random.key(seed), 7)
    queries = draw_queries(jax.random.fold_in(seeds[6], 71), 0)
    keys = draw_keys(jax.random.fold_in(seeds[6], 71), 0)
    values = scatter_about(seeds[2], (SEQUENCE_TOTAL, TOKENS_PER_SEQ, KEY_VALUE_HEADS * HEAD_SIZE), 1.0, 5.0, ((0, 8), (1, 4)))
    upstream_grad = scatter_about(seeds[3], (SEQUENCE_TOTAL, TOKENS_PER_SEQ, QUERY_HEAD_COUNT * HEAD_SIZE), (8 * (SEQUENCE_TOTAL * TOKENS_PER_SEQ) ** -0.5), 2.0, ((0, 8), (1, 4)))
    adapter_in = scatter_about(seeds[4], (SEQUENCE_TOTAL, TOKENS_PER_SEQ, R), 1.0, 6.0, ((0, 8), (1, 4)))
    doc_lengths = jax.vmap(lambda own: ragged(own, NDOC, TOKENS_PER_SEQ, DOC_MAX, 0))(jax.random.split(seeds[5], SEQUENCE_TOTAL)).reshape((SEQUENCE_TOTAL, NDOC)).astype(jnp.int32)
    return {"queries": queries, "keys": keys, "values": values, "upstream_grad": upstream_grad, "adapter_in": adapter_in, "doc_lengths": doc_lengths}


NEGATIVE = -1e+30
ROPE_BASE = 500000.0

def doc_layout(lengths, seq_length):
    ends = jnp.cumsum(lengths).astype(jnp.int32)
    places = jnp.arange(seq_length, dtype=jnp.int32)
    passed = (places[:, None] >= ends[None, :]).astype(jnp.int32)
    segment = lax.optimization_barrier(jnp.sum(passed, axis=1)).astype(jnp.int32)
    started = lax.optimization_barrier(jnp.sum(passed * lengths[None, :], axis=1)).astype(jnp.int32)
    return (segment, places - started)

def unrotate(grads, position):
    half = grads.shape[1] // 2
    freq = jnp.exp(jnp.arange(half, dtype=jnp.float32) * (-math.log(ROPE_BASE) / half))
    angle = position.astype(jnp.float32)[:, None] * freq[None, :]
    cosine = jnp.cos(angle)
    sine = jnp.sin(angle)
    first_half = grads[:, :half]
    second_half = grads[:, half:]
    return jnp.concatenate([first_half * cosine + second_half * sine, second_half * cosine - first_half * sine], axis=1)

def head_grads(query_mat, key_mat, value_mat, upstream, segment):
    seq_length, head_width = query_mat.shape
    q_block = min(512, seq_length)
    k_block = q_block // 4
    score_scale = 1.0 / math.sqrt(head_width)
    tile_count = seq_length // k_block

    def one_block(index, result):
        block_start = jnp.asarray(index, jnp.int32) * q_block
        query_blk = lax.dynamic_slice_in_dim(query_mat, block_start, q_block, 0)
        grad_blk = lax.dynamic_slice_in_dim(upstream, block_start, q_block, 0)
        seg_rows = lax.dynamic_slice_in_dim(segment, block_start, q_block, 0)
        row_ids = block_start + jnp.arange(q_block, dtype=jnp.int32)

        def tile_parts(tile):
            tile_start = jnp.asarray(tile, jnp.int32) * k_block
            key_tile = lax.dynamic_slice_in_dim(key_mat, tile_start, k_block, 0)
            value_tile = lax.dynamic_slice_in_dim(value_mat, tile_start, k_block, 0)
            seg_cols = lax.dynamic_slice_in_dim(segment, tile_start, k_block, 0)
            col_ids = tile_start + jnp.arange(k_block, dtype=jnp.int32)
            allowed = (col_ids[None, :] <= row_ids[:, None]) & (seg_cols[None, :] == seg_rows[:, None])
            is_live = (tile_start <= block_start + q_block - 1) & (seg_cols[k_block - 1] >= seg_rows[0])
            return (key_tile, value_tile, allowed, is_live)

        def masked_scores(key_tile, allowed):
            raw = jnp.dot(query_blk, key_tile.T, preferred_element_type=jnp.float32) * score_scale
            return jnp.where(allowed, raw, NEGATIVE)

        def stats_step(tile, carry):
            key_tile, value_tile, allowed, is_live = tile_parts(tile)

            def update(state):
                row_peak, row_total = state
                scores = masked_scores(key_tile, allowed)
                new_peak = jnp.maximum(row_peak, lax.optimization_barrier(jnp.max(scores, axis=1)))
                expo = jnp.where(allowed, jnp.exp(scores - new_peak[:, None]), 0.0)
                return (new_peak, row_total * jnp.exp(row_peak - new_peak) + lax.optimization_barrier(jnp.sum(expo, axis=1)))
            return lax.cond(is_live, update, lambda state: state, carry)
        start_stats = (jnp.full((q_block,), NEGATIVE, jnp.float32), jnp.zeros((q_block,), jnp.float32))
        row_peak, row_total = lax.fori_loop(0, tile_count, stats_step, start_stats)

        def grad_step(tile, carry):
            key_tile, value_tile, allowed, is_live = tile_parts(tile)

            def update(state):
                row_delta, acc_weighted, acc_plain = state
                scores = masked_scores(key_tile, allowed)
                softmax_w = jnp.where(allowed, jnp.exp(scores - row_peak[:, None]) / row_total[:, None], 0.0)
                grad_w = jnp.dot(grad_blk, value_tile.T, preferred_element_type=jnp.float32)
                weighted = softmax_w * grad_w
                stacked = jnp.concatenate([weighted.astype(jnp.bfloat16), softmax_w.astype(jnp.bfloat16)], axis=0)
                both = jnp.dot(stacked, key_tile, preferred_element_type=jnp.float32)
                return (row_delta + lax.optimization_barrier(jnp.sum(weighted, axis=1)), acc_weighted + both[:q_block], acc_plain + both[q_block:])
            return lax.cond(is_live, update, lambda state: state, carry)
        start_grads = (jnp.zeros((q_block,), jnp.float32), jnp.zeros((q_block, head_width), jnp.float32), jnp.zeros((q_block, head_width), jnp.float32))
        row_delta, acc_weighted, acc_plain = lax.fori_loop(0, tile_count, grad_step, start_grads)
        block_grad = (acc_weighted - row_delta[:, None] * acc_plain) * score_scale
        return lax.dynamic_update_slice_in_dim(result, block_grad, block_start, 0)
    return lax.fori_loop(0, seq_length // q_block, one_block, jnp.zeros((seq_length, head_width), jnp.float32))

def reference(queries, keys, values, upstream_grad, adapter_in, doc_lengths):

    def one_head(head):
        kv_head = head // GROUP

        def one_seq(running, seq_index):

            def columns(tensor_data, which):
                seq_rows = lax.dynamic_index_in_dim(tensor_data, seq_index, 0, keepdims=False)
                return lax.dynamic_slice_in_dim(seq_rows, which * HEAD_SIZE, HEAD_SIZE, 1)
            lengths = lax.dynamic_index_in_dim(doc_lengths, seq_index, 0, keepdims=False)
            segment, position = doc_layout(lengths, TOKENS_PER_SEQ)
            grads = head_grads(columns(queries, head), columns(keys, kv_head), columns(values, kv_head), columns(upstream_grad, head), segment)
            rotated = unrotate(grads, position).astype(jnp.bfloat16)
            inputs = lax.dynamic_index_in_dim(adapter_in, seq_index, 0, keepdims=False)
            return (running + jnp.dot(inputs.T, rotated, preferred_element_type=jnp.float32), None)
        summed, unused = lax.scan(one_seq, jnp.zeros((R, HEAD_SIZE), jnp.float32), jnp.arange(SEQUENCE_TOTAL, dtype=jnp.int32))
        return summed
    blocks = lax.map(one_head, jnp.arange(QUERY_HEAD_COUNT, dtype=jnp.int32))
    return jnp.transpose(blocks, (1, 0, 2)).reshape(R, QUERY_HEAD_COUNT * HEAD_SIZE)
```

```python
import functools
import math

import jax
import jax.numpy as jnp
from jax import lax
from jax.experimental import pallas as pl
from jax.experimental.pallas import tpu as pltpu
from jax.sharding import PartitionSpec as P

HEAD_SIZE = 128
GROUP = 8
NEGATIVE = -1e30
ROPE_BASE = 500000.0
LOG2E = 1.4426950408889634
MESH = pl.DeviceIdType.MESH


def when(cond, fn):
    if isinstance(cond, bool):
        if cond:
            fn()
    else:
        pl.when(cond)(fn)


def loop(count, body):
    if count <= 8:
        for i in range(count):
            body(i)
    else:
        lax.fori_loop(0, count, lambda i, c: (body(i), c)[1], 0)


def kernel(
    n, fs, dn, back, lengths, q_in, k_in, v_in, g_in, a_in, out,
    q, g, kc, vc, a, at, bias, cosw, sinw, dq,
    own, fsend, frecv, totf, totb, drecv, fin, zsend, zrecv, ag,
    local, kvs, kvr, fss, fsr, dps, dpr, zs, zr, ags, agr,
):
    z, f, d = lax.axis_index("seq"), lax.axis_index("fsdp"), lax.axis_index("dp")
    tokens, width = q.shape
    kv_heads = kc.shape[0]
    rank = a.shape[1]
    rows = rank // fs
    piece = rows // dn
    cols = width // n
    heads = cols // HEAD_SIZE
    group = width // HEAD_SIZE // kv_heads
    scale = 1.0 / math.sqrt(HEAD_SIZE)
    span = (back + 1) * tokens

    loads = [
        pltpu.make_async_copy(q_in.at[0], q, local.at[0]),
        pltpu.make_async_copy(g_in.at[0], g, local.at[1]),
        pltpu.make_async_copy(a_in.at[0], a, local.at[2]),
    ]
    for j in range(kv_heads):
        head = pl.ds(j * HEAD_SIZE, HEAD_SIZE)
        mine = pl.ds(back * tokens, tokens)
        loads.append(pltpu.make_async_copy(k_in.at[0, :, head], kc.at[j, mine], local.at[3 + 2 * j]))
        loads.append(pltpu.make_async_copy(v_in.at[0, :, head], vc.at[j, mine], local.at[4 + 2 * j]))
    for copy in loads:
        copy.start()

    barrier = pltpu.get_barrier_semaphore()
    for axis, me, size in (("seq", z, n), ("fsdp", f, fs), ("dp", d, dn)):
        for o in range(1, size):
            pl.semaphore_signal(
                barrier, inc=1, device_id={axis: lax.rem(me + o, size)}, device_id_type=MESH
            )
    pl.semaphore_wait(barrier, n + fs + dn - 3)

    def kv_copy(src, dst, which, j, p, to):
        head = pl.ds(pl.multiple_of(j * HEAD_SIZE, HEAD_SIZE), HEAD_SIZE)
        return pltpu.make_async_remote_copy(
            src_ref=src.at[0, :, head],
            dst_ref=dst.at[j, pl.ds((back - p) * tokens, tokens)],
            send_sem=kvs.at[which, j, p - 1],
            recv_sem=kvr.at[which, j, p - 1],
            device_id={"seq": to},
            device_id_type=MESH,
        )

    def first_kv(who):
        return lax.rem(who + 1, n) * heads // group

    for p in range(1, back + 1):
        @pl.when(z + p < n)
        def _(p=p):
            for i in range(kv_heads):
                j = lax.rem(first_kv(z + p) + i, kv_heads)
                kv_copy(k_in, kc, 0, j, p, z + p).start()
                kv_copy(v_in, vc, 1, j, p, z + p).start()

        @pl.when(z - p < 0)
        def _(p=p):
            block = pl.ds((back - p) * tokens, tokens)
            kc[:, block, :] = jnp.zeros((kv_heads, tokens, HEAD_SIZE), kc.dtype)
            vc[:, block, :] = jnp.zeros((kv_heads, tokens, HEAD_SIZE), vc.dtype)

    def layout(shape):
        place = z * tokens + lax.broadcasted_iota(jnp.int32, shape, 0)
        started = jnp.zeros(shape, jnp.int32)
        end = jnp.int32(0)
        for j in range(lengths.shape[1]):
            end = end + lengths[0, j]
            started = started + jnp.where(place >= end, lengths[0, j], 0)
        return place, started

    place, started = layout((tokens, span))
    key = (z - back) * tokens + lax.broadcasted_iota(jnp.int32, (tokens, span), 1)
    bias[...] = jnp.where((key >= started) & (key <= place), 0.0, NEGATIVE)
    place, started = layout((tokens, HEAD_SIZE))
    lane = lax.broadcasted_iota(jnp.int32, (tokens, HEAD_SIZE), 1)
    half = HEAD_SIZE // 2
    upper = lane >= half
    step = jnp.where(upper, lane - half, lane).astype(jnp.float32)
    freq = jnp.exp(step * (-math.log(ROPE_BASE) / half))
    angle = (place - started).astype(jnp.float32) * freq
    cosw[...] = jnp.cos(angle)
    sine = jnp.sin(angle)
    sinw[...] = jnp.where(upper, -sine, sine)

    loads[2].wait()
    at[...] = a[...].astype(jnp.float32).T
    turned = jnp.concatenate(
        [at[pl.ds(pl.multiple_of(lax.rem(f + o, fs) * rows, rows), rows), :] for o in range(fs)],
        axis=0,
    ).astype(jnp.bfloat16)
    for index, copy in enumerate(loads):
        if index != 2:
            copy.wait()

    def kv_arrived(j):
        for p in range(1, back + 1):
            @pl.when(z - p >= 0)
            def _(p=p):
                kv_copy(k_in, kc, 0, j, p, z + p).wait_recv()
                kv_copy(v_in, vc, 1, j, p, z + p).wait_recv()

    if heads != group:
        for j in range(kv_heads):
            kv_arrived(j)

    def block_of(i):
        return lax.rem(z + 1 + i, n)

    def fs_copy(i, o):
        return pltpu.make_async_remote_copy(
            src_ref=fsend.at[i, o - 1], dst_ref=frecv.at[i, o - 1],
            send_sem=fss.at[i, o - 1], recv_sem=fsr.at[i, o - 1],
            device_id={"fsdp": lax.rem(f + o, fs)}, device_id_type=MESH,
        )

    def dp_copy(i, o):
        peer = lax.rem(d + o, dn)
        return pltpu.make_async_remote_copy(
            src_ref=totb.at[i, peer], dst_ref=drecv.at[i, o - 1],
            send_sem=dps.at[i, o - 1], recv_sem=dpr.at[i, o - 1],
            device_id={"dp": peer}, device_id_type=MESH,
        )

    def z_copy(i):
        return pltpu.make_async_remote_copy(
            src_ref=zsend.at[i], dst_ref=zrecv.at[i],
            send_sem=zs.at[i], recv_sem=zr.at[i],
            device_id={"seq": block_of(i)}, device_id_type=MESH,
        )

    def ag_copy(o):
        return pltpu.make_async_remote_copy(
            src_ref=ag.at[d], dst_ref=ag.at[d],
            send_sem=ags.at[o - 1], recv_sem=agr.at[o - 1],
            device_id={"dp": lax.rem(d + o, dn)}, device_id_type=MESH,
        )

    def attend(i):
        block = block_of(i)
        j = block * heads // group
        if heads == group:
            kv_arrived(j)
        for h in range(heads):
            at_head = pl.ds(pl.multiple_of(block * cols + h * HEAD_SIZE, HEAD_SIZE), HEAD_SIZE)
            keys, vals = kc[j], vc[j]
            contract = (((1,), (1,)), ((), ()))
            raw = lax.dot_general(q[:, at_head], keys, contract, preferred_element_type=jnp.float32)
            grad = lax.dot_general(g[:, at_head], vals, contract, preferred_element_type=jnp.float32)
            score = raw * (scale * LOG2E) + bias[...]
            expo = jnp.exp2(score - jnp.max(score, axis=1, keepdims=True))
            prob = expo * (1.0 / jnp.sum(expo, axis=1, keepdims=True))
            weighted = prob * grad
            delta = jnp.sum(weighted, axis=1, keepdims=True)
            stacked = jnp.concatenate(
                [weighted.astype(jnp.bfloat16), prob.astype(jnp.bfloat16)], axis=0
            )
            both = jnp.dot(stacked, keys, preferred_element_type=jnp.float32)
            rot = (both[:tokens] - delta * both[tokens:]) * scale
            pre = rot * cosw[...] + pltpu.roll(rot, half, 1) * sinw[...]
            dq[:, h * HEAD_SIZE:(h + 1) * HEAD_SIZE] = pre.astype(jnp.bfloat16)
        term = jnp.dot(turned, dq[...], preferred_element_type=jnp.float32)
        own[i] = term[:rows]
        for o in range(1, fs):
            fsend[i, o - 1] = term[o * rows:(o + 1) * rows].astype(jnp.bfloat16)
            fs_copy(i, o).start()

    def over_dp(i):
        total = own[i]
        for o in range(1, fs):
            fs_copy(i, o).wait_recv()
            total = total + frecv[i, o - 1].astype(jnp.float32)
        for s in range(dn):
            part = total[s * piece:(s + 1) * piece]
            totf[i, s] = part
            totb[i, s] = part.astype(jnp.bfloat16)
        for o in range(1, dn):
            dp_copy(i, o).start()

    def over_z(i):
        total = totf[i, d]
        for o in range(1, dn):
            dp_copy(i, o).wait_recv()
            total = total + drecv[i, o - 1].astype(jnp.float32)

        def keep():
            fin[...] = total

        def send():
            zsend[i] = total.astype(jnp.bfloat16)
            z_copy(i).start()

        when(i == n - 1, keep)
        when(i != n - 1, send)

    def stage(i):
        when(i < n, lambda: attend(i))
        when((i >= 1) & (i <= n) if not isinstance(i, int) else 1 <= i <= n, lambda: over_dp(i - 1))
        when(i >= 2, lambda: over_z(i - 2))

    loop(n + 2, stage)

    total = fin[...]
    for i in range(n - 1):
        z_copy(i).wait_recv()
        total = total + zrecv[i].astype(jnp.float32)
    ag[d] = total.astype(ag.dtype)
    for o in range(1, dn):
        ag_copy(o).start()
    for o in range(1, dn):
        ag_copy(o).wait_recv()
    for s in range(dn):
        out[s * piece:(s + 1) * piece, :] = ag[s].astype(out.dtype)

    for p in range(1, back + 1):
        @pl.when(z + p < n)
        def _(p=p):
            for j in range(kv_heads):
                kv_copy(k_in, kc, 0, j, p, z + p).wait_send()
                kv_copy(v_in, vc, 1, j, p, z + p).wait_send()

    def sent(i):
        for o in range(1, fs):
            fs_copy(i, o).wait_send()
        for o in range(1, dn):
            dp_copy(i, o).wait_send()
        when(i < n - 1, lambda: z_copy(i).wait_send())

    loop(n, sent)
    for o in range(1, dn):
        ag_copy(o).wait_send()


def solution(mesh):
    n, fs, dn = mesh.shape["seq"], mesh.shape["fsdp"], mesh.shape["dp"]

    def per_device(queries, keys, values, upstream_grad, adapter_in, doc_lengths):
        _, tokens, width = queries.shape
        kv_heads = keys.shape[2] // HEAD_SIZE
        rank = adapter_in.shape[2]
        longest = 2 * tokens * n // doc_lengths.shape[1]
        back = min(n - 1, -(-(longest - 1) // tokens))
        span = (back + 1) * tokens
        rows, cols = rank // fs, width // n
        piece = rows // dn
        bf, f32 = jnp.bfloat16, jnp.float32
        dma = pltpu.SemaphoreType.DMA
        some = lambda k: max(k, 1)
        any_spec = pl.BlockSpec(memory_space=pl.ANY)
        return pl.pallas_call(
            functools.partial(kernel, n, fs, dn, back),
            out_shape=jax.ShapeDtypeStruct((rows, cols), f32),
            in_specs=[pl.BlockSpec(memory_space=pltpu.SMEM)] + [any_spec] * 5,
            out_specs=pl.BlockSpec(memory_space=pltpu.VMEM),
            scratch_shapes=[
                pltpu.VMEM((tokens, width), bf),
                pltpu.VMEM((tokens, width), bf),
                pltpu.VMEM((kv_heads, span, HEAD_SIZE), bf),
                pltpu.VMEM((kv_heads, span, HEAD_SIZE), bf),
                pltpu.VMEM((tokens, rank), bf),
                pltpu.VMEM((rank, tokens), f32),
                pltpu.VMEM((tokens, span), f32),
                pltpu.VMEM((tokens, HEAD_SIZE), f32),
                pltpu.VMEM((tokens, HEAD_SIZE), f32),
                pltpu.VMEM((tokens, cols), bf),
                pltpu.VMEM((n, rows, cols), f32),
                pltpu.VMEM((n, some(fs - 1), rows, cols), bf),
                pltpu.VMEM((n, some(fs - 1), rows, cols), bf),
                pltpu.VMEM((n, dn, piece, cols), f32),
                pltpu.VMEM((n, dn, piece, cols), bf),
                pltpu.VMEM((n, some(dn - 1), piece, cols), bf),
                pltpu.VMEM((piece, cols), f32),
                pltpu.VMEM((some(n - 1), piece, cols), bf),
                pltpu.VMEM((some(n - 1), piece, cols), bf),
                pltpu.VMEM((dn, piece, cols), bf),
                dma((3 + 2 * kv_heads,)),
                dma((2, kv_heads, some(back))),
                dma((2, kv_heads, some(back))),
                dma((n, some(fs - 1))),
                dma((n, some(fs - 1))),
                dma((n, some(dn - 1))),
                dma((n, some(dn - 1))),
                dma((some(n - 1),)),
                dma((some(n - 1),)),
                dma((some(dn - 1),)),
                dma((some(dn - 1),)),
            ],
            compiler_params=pltpu.CompilerParams(collective_id=0, has_side_effects=True),
        )(doc_lengths, queries, keys, values, upstream_grad, adapter_in)

    return jax.shard_map(
        per_device,
        mesh=mesh,
        in_specs=(P(("dp", "fsdp"), "seq", None),) * 5 + (P(("dp", "fsdp"), None),),
        out_specs=P("fsdp", "seq"),
        check_vma=False,
    )
```

```python
import functools
import math

import jax
import jax.numpy as jnp
from jax import lax
from jax.experimental import pallas as pl
from jax.experimental.pallas import tpu as pltpu
from jax.sharding import PartitionSpec as P

HEAD_SIZE = 128
SPLIT = 1
FIRST_LAG = 1
SECOND_LAG = 3
NEGATIVE = -1e30
ROPE_BASE = 500000.0
LOG2E = 1.4426950408889634
MESH = pl.DeviceIdType.MESH


def when(cond, fn):
    if isinstance(cond, bool):
        if cond:
            fn()
    else:
        pl.when(cond)(fn)


def loop(count, body):
    if count <= 24:
        for i in range(count):
            body(i)
    else:
        lax.fori_loop(0, count, lambda i, c: (body(i), c)[1], 0)


def kernel(
    n, fs, dn, back, lengths, q_in, k_in, v_in, g_in, a_in, out,
    q, g, kc, vc, kt, vt, a, at, bias, low, cosw, sinw, dq,
    own, fsend, frecv, totf, totb, drecv, fin, zsend, zrecv, ag,
    local, kvs, kvr, fss, fsr, dps, dpr, zs, zr, ags, agr,
):
    z, f, d = lax.axis_index("seq"), lax.axis_index("fsdp"), lax.axis_index("dp")
    tokens, width = q.shape
    kv_heads = kc.shape[0]
    rank = a.shape[1]
    rows = rank // fs
    piece = rows // dn
    subs = fin.shape[0]
    cols = width // n // subs
    heads = cols // HEAD_SIZE
    whole = subs * heads
    steps = n * subs
    group = width // HEAD_SIZE // kv_heads
    scale = 1.0 / math.sqrt(HEAD_SIZE)
    batch = min(4, heads)
    span = (back + 1) * tokens

    loads = [
        pltpu.make_async_copy(q_in.at[0], q, local.at[0]),
        pltpu.make_async_copy(g_in.at[0], g, local.at[1]),
        pltpu.make_async_copy(a_in.at[0], a, local.at[2]),
    ]
    for j in range(kv_heads):
        head = pl.ds(j * HEAD_SIZE, HEAD_SIZE)
        mine = pl.ds(back * tokens, tokens)
        loads.append(pltpu.make_async_copy(k_in.at[0, :, head], kc.at[j, mine], local.at[3 + 2 * j]))
        loads.append(pltpu.make_async_copy(v_in.at[0, :, head], vc.at[j, mine], local.at[4 + 2 * j]))
    for copy in loads:
        copy.start()

    barrier = pltpu.get_barrier_semaphore()
    for axis, me, size in (("seq", z, n), ("fsdp", f, fs), ("dp", d, dn)):
        for o in range(1, size):
            pl.semaphore_signal(
                barrier, inc=1, device_id={axis: lax.rem(me + o, size)}, device_id_type=MESH
            )
    pl.semaphore_wait(barrier, n + fs + dn - 3)

    def kv_copy(src, dst, which, j, p, to):
        head = pl.ds(pl.multiple_of(j * HEAD_SIZE, HEAD_SIZE), HEAD_SIZE)
        return pltpu.make_async_remote_copy(
            src_ref=src.at[0, :, head],
            dst_ref=dst.at[j, pl.ds((back - p) * tokens, tokens)],
            send_sem=kvs.at[which, j, p - 1],
            recv_sem=kvr.at[which, j, p - 1],
            device_id={"seq": to},
            device_id_type=MESH,
        )

    def first_kv(who):
        return lax.rem(who + 1, n) * whole // group

    for p in range(1, back + 1):
        @pl.when(z + p < n)
        def _(p=p):
            for i in range(kv_heads):
                j = lax.rem(first_kv(z + p) + i, kv_heads)
                kv_copy(k_in, kc, 0, j, p, z + p).start()
                kv_copy(v_in, vc, 1, j, p, z + p).start()

        @pl.when(z - p < 0)
        def _(p=p):
            block = pl.ds((back - p) * tokens, tokens)
            kc[:, block, :] = jnp.zeros((kv_heads, tokens, HEAD_SIZE), kc.dtype)
            vc[:, block, :] = jnp.zeros((kv_heads, tokens, HEAD_SIZE), vc.dtype)

    def layout(shape):
        place = z * tokens + lax.broadcasted_iota(jnp.int32, shape, 0)
        started = jnp.zeros(shape, jnp.int32)
        end = jnp.int32(0)
        for j in range(lengths.shape[1]):
            end = end + lengths[0, j]
            started = started + jnp.where(place >= end, lengths[0, j], 0)
        return place, started

    wide = (tokens, span - tokens)
    place, started = layout(wide)
    column = lax.broadcasted_iota(jnp.int32, wide, 1)
    key = (z - back) * tokens + column
    key = jnp.where(column <= place - z * tokens, key + back * tokens, key) if back == 1 else (
        jnp.where((column < tokens) & (column <= place - z * tokens), key + back * tokens, key)
    )
    bias[...] = jnp.where(key >= started, 0.0, NEGATIVE)
    square = (tokens, tokens)
    lower = lax.broadcasted_iota(jnp.int32, square, 1) <= lax.broadcasted_iota(jnp.int32, square, 0)
    low[...] = jnp.where(lower, 1.0, 0.0).astype(jnp.bfloat16)

    def fold(x):
        first = jnp.where(lower, x[:, span - tokens:], x[:, :tokens])
        if back == 1:
            return first
        return jnp.concatenate([first, x[:, tokens:span - tokens]], axis=1)

    def unfold(x):
        mine = x[:, :tokens] * low[...]
        return jnp.concatenate([x[:, :tokens] - mine, x[:, tokens:], mine] if back > 1
                               else [x - mine, mine], axis=1)

    place, started = layout((tokens, HEAD_SIZE))
    lane = lax.broadcasted_iota(jnp.int32, (tokens, HEAD_SIZE), 1)
    half = HEAD_SIZE // 2
    upper = lane >= half
    step = jnp.where(upper, lane - half, lane).astype(jnp.float32)
    freq = jnp.exp(step * (-math.log(ROPE_BASE) / half))
    angle = (place - started).astype(jnp.float32) * freq
    cosw[...] = jnp.cos(angle) * scale
    sine = jnp.sin(angle) * scale
    sinw[...] = jnp.where(upper, -sine, sine)

    loads[2].wait()
    at[...] = a[...].astype(jnp.float32).T
    turned = jnp.concatenate(
        [at[pl.ds(pl.multiple_of(lax.rem(f + o, fs) * rows, rows), rows), :] for o in range(fs)],
        axis=0,
    ).astype(jnp.bfloat16)
    for index, copy in enumerate(loads):
        if index != 2:
            copy.wait()

    def kv_arrived(j):
        for p in range(1, back + 1):
            @pl.when(z - p >= 0)
            def _(p=p):
                kv_copy(k_in, kc, 0, j, p, z + p).wait_recv()
                kv_copy(v_in, vc, 1, j, p, z + p).wait_recv()

    if whole != group:
        for j in range(kv_heads):
            kv_arrived(j)

    def block_of(i):
        return lax.rem(z + 1 + i // subs, n)

    def fs_copy(i, o):
        return pltpu.make_async_remote_copy(
            src_ref=fsend.at[i, o - 1], dst_ref=frecv.at[i, o - 1],
            send_sem=fss.at[i, o - 1], recv_sem=fsr.at[i, o - 1],
            device_id={"fsdp": lax.rem(f + o, fs)}, device_id_type=MESH,
        )

    def dp_copy(i, o):
        peer = lax.rem(d + o, dn)
        return pltpu.make_async_remote_copy(
            src_ref=totb.at[i, peer], dst_ref=drecv.at[i, o - 1],
            send_sem=dps.at[i, o - 1], recv_sem=dpr.at[i, o - 1],
            device_id={"dp": peer}, device_id_type=MESH,
        )

    def z_copy(i):
        return pltpu.make_async_remote_copy(
            src_ref=zsend.at[i], dst_ref=zrecv.at[i],
            send_sem=zs.at[i], recv_sem=zr.at[i],
            device_id={"seq": block_of(i)}, device_id_type=MESH,
        )

    def ag_copy(s, o):
        return pltpu.make_async_remote_copy(
            src_ref=ag.at[s, d], dst_ref=ag.at[s, d],
            send_sem=ags.at[s, o - 1], recv_sem=agr.at[s, o - 1],
            device_id={"dp": lax.rem(d + o, dn)}, device_id_type=MESH,
        )

    def attend(i):
        block = block_of(i)
        j = block * whole // group

        def keys_in():
            if whole == group:
                kv_arrived(j)
            kt[...] = kc[j].T
            vt[...] = vc[j].T

        when(i % subs == 0, keys_in)
        start = block * subs * cols + (i % subs) * cols
        for h in range(0, heads, batch):
            def rows_of(ref):
                return jnp.concatenate([
                    ref[:, pl.ds(pl.multiple_of(start + e * HEAD_SIZE, HEAD_SIZE), HEAD_SIZE)]
                    for e in range(h, h + batch)
                ], axis=0)

            raw = jnp.dot(rows_of(q), kt[...], preferred_element_type=jnp.float32)
            grad = jnp.dot(rows_of(g), vt[...], preferred_element_type=jnp.float32)
            parts, deltas = [], []
            for e in range(batch):
                mine = slice(e * tokens, (e + 1) * tokens)
                score = fold(raw[mine]) * (scale * LOG2E) + bias[...]
                expo = jnp.exp2(score - jnp.max(score, axis=1, keepdims=True))
                prob = expo * (1.0 / jnp.sum(expo, axis=1, keepdims=True))
                weighted = prob * fold(grad[mine])
                deltas.append(jnp.sum(weighted, axis=1, keepdims=True))
                parts.append(unfold(weighted.astype(jnp.bfloat16)))
                parts.append(unfold(prob.astype(jnp.bfloat16)))
            both = jnp.dot(jnp.concatenate(parts, axis=0), kc[j], preferred_element_type=jnp.float32)
            for e in range(batch):
                base = 2 * e * tokens
                rot = both[base:base + tokens] - deltas[e] * both[base + tokens:base + 2 * tokens]
                pre = rot * cosw[...] + pltpu.roll(rot, half, 1) * sinw[...]
                dq[:, (h + e) * HEAD_SIZE:(h + e + 1) * HEAD_SIZE] = pre.astype(jnp.bfloat16)
        term = jnp.dot(turned, dq[...], preferred_element_type=jnp.float32)
        own[i] = term[:rows]
        for o in range(1, fs):
            fsend[i, o - 1] = term[o * rows:(o + 1) * rows].astype(jnp.bfloat16)
            fs_copy(i, o).start()

    def over_dp(i):
        total = own[i]
        for o in range(1, fs):
            fs_copy(i, o).wait_recv()
            total = total + frecv[i, o - 1].astype(jnp.float32)
        for s in range(dn):
            part = total[s * piece:(s + 1) * piece]
            totf[i, s] = part
            totb[i, s] = part.astype(jnp.bfloat16)
        for o in range(1, dn):
            dp_copy(i, o).start()

    def over_z(i):
        total = totf[i, d]
        for o in range(1, dn):
            dp_copy(i, o).wait_recv()
            total = total + drecv[i, o - 1].astype(jnp.float32)

        def send():
            zsend[i] = total.astype(jnp.bfloat16)
            z_copy(i).start()

        def share():
            sub = i - (n - 1) * subs
            done = total
            for k in range(n - 1):
                z_copy(k * subs + sub).wait_recv()
                done = done + zrecv[k * subs + sub].astype(jnp.float32)
            ag[sub, d] = done.astype(ag.dtype)
            for o in range(1, dn):
                ag_copy(sub, o).start()

        when(i < (n - 1) * subs, send)
        when(i >= (n - 1) * subs, share)

    def stage(i):
        def at_step(k, fn):
            if isinstance(k, int):
                when(0 <= k < steps, lambda: fn(k))
            else:
                when((k >= 0) & (k < steps), lambda: fn(k))

        at_step(i, attend)
        at_step(i - FIRST_LAG, over_dp)
        at_step(i - SECOND_LAG, over_z)

    loop(steps + SECOND_LAG, stage)

    for s in range(subs):
        for o in range(1, dn):
            ag_copy(s, o).wait_recv()
        for r in range(dn):
            out[r * piece:(r + 1) * piece, s * cols:(s + 1) * cols] = ag[s, r].astype(out.dtype)

    for p in range(1, back + 1):
        @pl.when(z + p < n)
        def _(p=p):
            for j in range(kv_heads):
                kv_copy(k_in, kc, 0, j, p, z + p).wait_send()
                kv_copy(v_in, vc, 1, j, p, z + p).wait_send()

    def sent(i):
        for o in range(1, fs):
            fs_copy(i, o).wait_send()
        for o in range(1, dn):
            dp_copy(i, o).wait_send()
        when(i < (n - 1) * subs, lambda: z_copy(i).wait_send())

    loop(steps, sent)
    for s in range(subs):
        for o in range(1, dn):
            ag_copy(s, o).wait_send()


def solution(mesh):
    n, fs, dn = mesh.shape["seq"], mesh.shape["fsdp"], mesh.shape["dp"]

    def per_device(queries, keys, values, upstream_grad, adapter_in, doc_lengths):
        _, tokens, width = queries.shape
        kv_heads = keys.shape[2] // HEAD_SIZE
        rank = adapter_in.shape[2]
        longest = 2 * tokens * n // doc_lengths.shape[1]
        back = -(-longest // tokens)
        span = (back + 1) * tokens
        subs = math.gcd(SPLIT, width // n // HEAD_SIZE)
        steps = n * subs
        rows, cols = rank // fs, width // n // subs
        piece = rows // dn
        bf, f32 = jnp.bfloat16, jnp.float32
        dma = pltpu.SemaphoreType.DMA
        some = lambda k: max(k, 1)
        any_spec = pl.BlockSpec(memory_space=pl.ANY)
        return pl.pallas_call(
            functools.partial(kernel, n, fs, dn, back),
            out_shape=jax.ShapeDtypeStruct((rows, width // n), f32),
            in_specs=[pl.BlockSpec(memory_space=pltpu.SMEM)] + [any_spec] * 5,
            out_specs=pl.BlockSpec(memory_space=pltpu.VMEM),
            scratch_shapes=[
                pltpu.VMEM((tokens, width), bf),
                pltpu.VMEM((tokens, width), bf),
                pltpu.VMEM((kv_heads, span, HEAD_SIZE), bf),
                pltpu.VMEM((kv_heads, span, HEAD_SIZE), bf),
                pltpu.VMEM((HEAD_SIZE, span), bf),
                pltpu.VMEM((HEAD_SIZE, span), bf),
                pltpu.VMEM((tokens, rank), bf),
                pltpu.VMEM((rank, tokens), f32),
                pltpu.VMEM((tokens, span - tokens), f32),
                pltpu.VMEM((tokens, tokens), bf),
                pltpu.VMEM((tokens, HEAD_SIZE), f32),
                pltpu.VMEM((tokens, HEAD_SIZE), f32),
                pltpu.VMEM((tokens, cols), bf),
                pltpu.VMEM((steps, rows, cols), f32),
                pltpu.VMEM((steps, some(fs - 1), rows, cols), bf),
                pltpu.VMEM((steps, some(fs - 1), rows, cols), bf),
                pltpu.VMEM((steps, dn, piece, cols), f32),
                pltpu.VMEM((steps, dn, piece, cols), bf),
                pltpu.VMEM((steps, some(dn - 1), piece, cols), bf),
                pltpu.VMEM((subs, piece, cols), f32),
                pltpu.VMEM((some(steps - subs), piece, cols), bf),
                pltpu.VMEM((some(steps - subs), piece, cols), bf),
                pltpu.VMEM((subs, dn, piece, cols), bf),
                dma((3 + 2 * kv_heads,)),
                dma((2, kv_heads, some(back))),
                dma((2, kv_heads, some(back))),
                dma((steps, some(fs - 1))),
                dma((steps, some(fs - 1))),
                dma((steps, some(dn - 1))),
                dma((steps, some(dn - 1))),
                dma((some(steps - subs),)),
                dma((some(steps - subs),)),
                dma((subs, some(dn - 1))),
                dma((subs, some(dn - 1))),
            ],
            compiler_params=pltpu.CompilerParams(collective_id=0, has_side_effects=True),
        )(doc_lengths, queries, keys, values, upstream_grad, adapter_in)

    return jax.shard_map(
        per_device,
        mesh=mesh,
        in_specs=(P(("dp", "fsdp"), "seq", None),) * 5 + (P(("dp", "fsdp"), None),),
        out_specs=P("fsdp", "seq"),
        check_vma=False,
    )
```
